32 devices in a mesh: ctx: 8 (over z, x), ep: 4 (over y, core).
Axes of the slice: x: 2, y: 2, z: 4, core: 2. Of those that a mesh axis runs over, the one named last changes fastest.
Arguments:
- queries: bfloat16 [4096, 2048], P('ctx', 'ep'), may hold values from -8 to 8
- keys: bfloat16 [4096, 2048], P('ctx', 'ep'), may hold values from -8 to 8
- values: bfloat16 [4096, 2048], P('ctx', 'ep'), may hold values from -6 to 6
- segments: int32 [4096], replicated, may hold values from 0 to 2, as said below
- residual: bfloat16 [4096, 2048], P(('ctx', 'ep')), may hold values from -6 to 6
- out_weight: bfloat16 [2048, 2048], P('ep'), may hold values from -0.125 to 0.125
- norm_gain: float32 [2048], replicated, may hold values from 0.1 to 1.9
- router: float32 [2048, 8], replicated, may hold values from -0.125 to 0.125
- routes: int32 [4096, 6], P(('ctx', 'ep')), may hold values from 0 to 7, all different within a row; in each aligned block of 128 rows (0 to 127, 128 to 255, ...) at most 128 rows name the same one
- gate_weight: bfloat16 [4, 8, 2048, 352], P('ep', 'ctx'), may hold values from -0.125 to 0.125
- up_weight: bfloat16 [4, 8, 2048, 352], P('ep', 'ctx'), may hold values from -0.125 to 0.125
- down_weight: bfloat16 [4, 8, 352, 2048], P('ep', 'ctx'), may hold values from -0.15625 to 0.15625
Outputs:
- layer_out: bfloat16 [4096, 2048], P(('ctx', 'ep'))
The draws below stay inside these ranges and needn't reach their ends.
Inputs may be any that keep to these rules, and one draw needn't show every extreme that they name: In each aligned block of 128 rows (the rows of one device), no expert is named by more than 128 routes; each row names 6 different experts. `segments`: segment ids start at 0 and never fall along the window.
All inputs are finite; a program needn't handle non-finite values.
Results may differ from the reference program's by a relative error of at most 0.0075.
Values may be sent and summed in bfloat16 or wider, within the bound.
No kernel may reach another device: no remote copies, remote signals or barrier semaphores. Data moves between devices by JAX's collectives and lax.ppermute only.
A program may use at most 128 MiB of HBM per device.

```python
import math
import jax
import jax.numpy as jnp
import numpy as np
from jax import lax

D = 2048
H = 16
HD = 128
FF = 1408
TOPK = 6
SPLIT = 4
SEQ = 4096
TOK = 128
EXPERTS = 8
FFQ = 352
CAP = 128
N_CTX = 8
N_EP = 4


def base_noise(key):
    return jnp.clip(1.5 * jax.random.normal(key, (SEQ, H * HD)), -6.0, 6.0)


def draw_queries(key, part):
    noise = base_noise(jax.random.fold_in(key, 1))
    return noise.astype(jnp.bfloat16)


def draw_keys(key, part):
    noise = base_noise(jax.random.fold_in(key, 2))
    return noise.astype(jnp.bfloat16)


def draw_segments(key, part):
    lower = jax.random.randint(jax.random.fold_in(key, 21), (), 1, SEQ // 4)
    upper = SEQ - jax.random.randint(jax.random.fold_in(key, 22), (), 1, SEQ // 4)
    positions = jnp.arange(SEQ, dtype=jnp.int32)
    return ((positions >= lower).astype(jnp.int32) + (positions >= upper).astype(jnp.int32)).astype(jnp.int32)


def levels(key, extent, cuts, low, largest):
    def one(dim, blocks):
        heights = jax.random.uniform(jax.random.fold_in(jax.random.fold_in(key, 6), dim), (blocks,), jnp.float32, low / len(cuts), largest / len(cuts))
        return jnp.repeat(jnp.exp(heights), extent[dim] // blocks).reshape((-1,) + (1,) * (len(extent) - dim - 1))

    factor_of = one(*cuts[0])
    for cut in cuts[1:]:
        factor_of = factor_of * one(*cut)
    return factor_of


def deal_out(key, own, number, rows, number_of, top, most, slope):
    ranking = jax.random.permutation(key, number_of)
    crowded, common = shares(number_of, rows * top, most, slope, True), shares(number_of, rows * top, most, slope, False)
    places = jnp.arange(number_of)

    def named(tallies, turn):
        used = int((tallies > 0).sum())
        fixed = max(1, used // 4)
        shifted = fixed + (places - fixed + turn * (used - fixed)) % max(1, number_of - fixed)
        return jnp.zeros((number_of,), jnp.int32).at[ranking[jnp.where(places < fixed, places, shifted)]].set(jnp.asarray(tallies, jnp.int32))

    tallies = jnp.where(number % 4 == 0, named(crowded, number // 4), named(common, number - number // 4 - 1))
    mixed = jax.random.permutation(jax.random.fold_in(own, 3), number_of)
    source_of, receiver = mixed[0:number_of // 2 * 2:2], mixed[1:number_of // 2 * 2:2]
    slack = jnp.minimum(tallies[source_of] - 1, most - tallies[receiver]) // 2
    slack = jnp.where((source_of == ranking[0]) | (receiver == ranking[0]) | (tallies[receiver] == 0), 0, jnp.maximum(slack, 0))
    shifted = jax.random.randint(jax.random.fold_in(own, 4), (number_of // 2,), 0, 1 << 20) % (slack + 1)
    tallies = tallies.at[source_of].add(-shifted).at[receiver].add(shifted)
    items = jnp.searchsorted(jnp.cumsum(tallies), jnp.arange(rows * top), side="right").astype(jnp.int32)
    table = items.reshape(top, rows).T
    table = table[jax.random.permutation(jax.random.fold_in(own, 1), rows)]
    turn = jax.random.randint(jax.random.fold_in(own, 2), (rows, 1), 0, top)
    return jnp.take_along_axis(table, (jnp.arange(top)[None, :] + turn) % top, axis=1)


def shares(number_of, total, limit, lean, full):
    loads = [(1 << 20) // math.isqrt(grade ** lean) + 1 for grade in range(1, number_of + 1)]
    largest = limit if full else min(limit, max(-(-total // number_of), total * loads[0] // sum(loads)))
    least = 1 if total - largest >= number_of - 1 else 0
    counts, rest = [largest] + [least] * (number_of - 1), total - largest - least * (number_of - 1)
    while rest > 0:
        free = [i for i in range(1, number_of) if counts[i] < largest] or [i for i in range(1, number_of) if counts[i] < limit]
        pool, budget = sum([loads[i] for i in free]), rest
        for i in free:
            addition = min(limit - counts[i], max(1, budget * loads[i] // pool), rest)
            counts[i] = counts[i] + addition
            rest = rest - addition
    return np.array(counts)


def gaussian(own_key, dims, width, most, pieces=(), held_as=jnp.bfloat16):
    gain = levels(own_key, dims, pieces, -0.22, 0.18) if pieces else 1.0
    result = jax.random.normal(own_key, dims, jnp.float32) * width * gain
    return jnp.minimum(jnp.maximum(result, -most), most).astype(held_as)


def setup_inputs(seed: int = 0) -> dict:
    key_of = jax.random.split(jax.random.key(seed), 13)
    queries = draw_queries(jax.random.fold_in(key_of[12], 71), 0)
    keys = draw_keys(jax.random.fold_in(key_of[12], 71), 0)
    values = gaussian(key_of[2], (SEQ, H * HD), 1.0, 6.0, ((0, 8), (1, 4)))
    segments = draw_segments(jax.random.fold_in(key_of[12], 71), 0)
    residual = gaussian(key_of[4], (SEQ, D), 1.0, 6.0, ((0, 32),))
    out_weight = gaussian(key_of[5], (H * HD, D), (H * HD) ** -0.5, 0.125, ((0, 4),))
    norm_gain = jnp.clip(1.0 + 0.18 * jax.random.normal(key_of[6], (D,), jnp.float32), 0.1, 1.9)
    router = gaussian(key_of[7], (D, EXPERTS), D ** -0.5, 0.125, (), jnp.float32)
    routes_keys = jax.random.split(jax.random.fold_in(key_of[8], 1), SEQ // TOK)
    routes_turns = jax.random.permutation(jax.random.fold_in(key_of[8], 3), SEQ // TOK)
    routes = jax.vmap(lambda own, number: deal_out(jax.random.fold_in(key_of[8], 2), own, number, TOK, EXPERTS, TOPK, CAP, 2))(routes_keys, routes_turns).reshape((SEQ, TOPK))
    gate_weight = gaussian(key_of[9], (N_EP, N_CTX, D, FFQ), D ** -0.5, 0.125, ((0, 4), (1, 8)))
    up_weight = gaussian(key_of[10], (N_EP, N_CTX, D, FFQ), D ** -0.5, 0.125, ((0, 4), (1, 8)))
    down_weight = gaussian(key_of[11], (N_EP, N_CTX, FFQ, D), FF ** -0.5, 0.15625, ((0, 4), (1, 8)))
    return {"queries": queries, "keys": keys, "values": values, "segments": segments, "residual": residual, "out_weight": out_weight, "norm_gain": norm_gain, "router": router, "routes": routes, "gate_weight": gate_weight, "up_weight": up_weight, "down_weight": down_weight}


def attend_head(query_h, key_h, value_h, segments):
    positions = jnp.arange(SEQ)
    block = 512 if SEQ % 512 == 0 else SEQ
    scale = HD ** (-0.5)

    def one_block(start):
        q_block = lax.dynamic_slice_in_dim(query_h, start, block)
        q_pos = start + jnp.arange(block)
        q_seg = lax.dynamic_slice_in_dim(segments, start, block)
        scores = jnp.dot(q_block, key_h.T, preferred_element_type=jnp.float32) * scale
        allowed = (q_seg[:, None] == segments[None, :]) & (positions[None, :] <= q_pos[:, None])
        scores = jnp.where(allowed, scores, jnp.float32(-1e+30))
        best = lax.optimization_barrier(jnp.max(scores, axis=1, keepdims=True))
        expo = jnp.where(allowed, jnp.exp(scores - best), jnp.float32(0.0))
        total = lax.optimization_barrier(jnp.sum(expo, axis=1, keepdims=True))
        probs = expo.astype(jnp.bfloat16)
        summed = jnp.dot(probs, value_h, preferred_element_type=jnp.float32)
        return (summed / total).astype(jnp.bfloat16)
    starts = (jnp.arange(SEQ // block) * block).astype(jnp.int32)
    return lax.map(one_block, starts).reshape(SEQ, HD)

def reference(queries, keys, values, segments, residual, out_weight, norm_gain, router, routes, gate_weight, up_weight, down_weight):
    query_t = jnp.transpose(queries.reshape(SEQ, H, HD), (1, 0, 2))
    key_t = jnp.transpose(keys.reshape(SEQ, H, HD), (1, 0, 2))
    value_t = jnp.transpose(values.reshape(SEQ, H, HD), (1, 0, 2))
    heads = lax.map(lambda item: attend_head(item[0], item[1], item[2], segments), (query_t, key_t, value_t))
    attended = jnp.transpose(heads, (1, 0, 2)).reshape(SEQ, H * HD)
    attn = jnp.dot(attended, out_weight, preferred_element_type=jnp.float32)
    stream = residual.astype(jnp.float32) + attn
    normed = (stream * lax.rsqrt(lax.optimization_barrier(jnp.mean(stream * stream, axis=1, keepdims=True)) + 1e-06) * norm_gain).astype(jnp.bfloat16)
    logits = jnp.dot(normed.astype(jnp.float32), router, precision=lax.Precision.HIGHEST)
    gates = jax.nn.sigmoid(jnp.take_along_axis(logits, routes, axis=1))
    weights = gates / lax.optimization_barrier(jnp.sum(gates, axis=1, keepdims=True))
    blocks = SEQ // TOK
    flat = routes.reshape(blocks, TOK * TOPK)
    onehot = (flat[:, :, None] == jnp.arange(EXPERTS, dtype=jnp.int32)[None, None, :]).astype(jnp.int32)
    before = jnp.cumsum(onehot, axis=1).astype(jnp.int32) - onehot
    rank = lax.optimization_barrier(jnp.sum(before * onehot, axis=2)).astype(jnp.int32)
    block_ids = jnp.broadcast_to(jnp.arange(blocks, dtype=jnp.int32)[:, None], (blocks, TOK * TOPK))
    token_ids = (block_ids * TOK + (jnp.arange(TOK * TOPK, dtype=jnp.int32) // TOPK)[None, :]).astype(jnp.int32)
    token_table = jnp.full((blocks, EXPERTS, CAP), SEQ, dtype=jnp.int32).at[block_ids, flat, rank].set(token_ids)
    weight_table = jnp.zeros((blocks, EXPERTS, CAP), jnp.float32).at[block_ids, flat, rank].set(weights.reshape(blocks, TOK * TOPK))
    normed_pad = jnp.concatenate([normed, jnp.zeros((1, D), jnp.bfloat16)], axis=0)
    gate_all = gate_weight.reshape(EXPERTS, SPLIT, D, FFQ)
    up_all = up_weight.reshape(EXPERTS, SPLIT, D, FFQ)
    down_all = down_weight.reshape(EXPERTS, SPLIT, FFQ, D)

    def one_expert(mixed, expert):
        index_rows = token_table[:, expert, :].reshape(-1)
        scale_rows = weight_table[:, expert, :].reshape(-1)
        rows = normed_pad[index_rows]
        total = jnp.zeros((rows.shape[0], D), jnp.float32)
        for piece in range(SPLIT):
            gate = jnp.dot(rows, gate_all[expert, piece], preferred_element_type=jnp.float32)
            upper = jnp.dot(rows, up_all[expert, piece], preferred_element_type=jnp.float32)
            act = (jax.nn.silu(gate) * upper).astype(jnp.bfloat16)
            part = jnp.dot(act, down_all[expert, piece], preferred_element_type=jnp.float32).astype(jnp.bfloat16)
            total = total + part.astype(jnp.float32)
        expert_out = total.astype(jnp.bfloat16).astype(jnp.float32)
        mixed = mixed.at[index_rows].add(scale_rows[:, None] * expert_out)
        return (mixed, None)
    mixed, _ = lax.scan(one_expert, jnp.zeros((SEQ + 1, D), jnp.float32), jnp.arange(EXPERTS, dtype=jnp.int32))
    return (stream + mixed[:SEQ]).astype(jnp.bfloat16)
```

```python
import functools

import jax
import jax.numpy as jnp
from jax import lax
from jax.experimental import pallas as pl
from jax.experimental.pallas import tpu as pltpu
from jax.sharding import PartitionSpec as P

HD = 128

def general_body(
    queries,
    keys,
    values,
    segments,
    residual,
    out_weight,
    norm_gain,
    router,
    routes,
    gate_weight,
    up_weight,
    down_weight,
):
    rows_ctx = queries.shape[0]
    width_heads = queries.shape[1]
    heads_dev = width_heads // HD
    model_width = residual.shape[1]
    tok_rows = residual.shape[0]
    n_ctx = lax.axis_size("ctx")
    n_ep = lax.axis_size("ep")
    first = lax.axis_index("ctx") * rows_ctx
    q_pos = first + jnp.arange(rows_ctx, dtype=jnp.int32)
    q_seg = lax.dynamic_slice_in_dim(segments, first, rows_ctx)
    q_heads = queries.reshape(rows_ctx, heads_dev, HD)
    scale = HD ** (-0.5)
    start_state = (
        jnp.full((heads_dev, rows_ctx), -1e30, jnp.float32),
        jnp.zeros((heads_dev, rows_ctx), jnp.float32),
        jnp.zeros((rows_ctx, heads_dev, HD), jnp.float32),
    )
    key_rows = lax.all_gather(keys, "ctx", axis=0, tiled=True)
    value_rows = lax.all_gather(values, "ctx", axis=0, tiled=True)
    count = key_rows.shape[0]
    width = 512

    def one_block(step, state):
        best, total, acc = state
        offset = step * width
        key_block = lax.dynamic_slice_in_dim(key_rows, offset, width).reshape(width, heads_dev, HD)
        value_block = lax.dynamic_slice_in_dim(value_rows, offset, width).reshape(
            width, heads_dev, HD
        )
        k_pos = offset + jnp.arange(width, dtype=jnp.int32)
        k_seg = lax.dynamic_slice_in_dim(segments, offset, width)
        allowed = (q_seg[:, None] == k_seg[None, :]) & (k_pos[None, :] <= q_pos[:, None])
        scores = (
            jnp.einsum("qhd,khd->hqk", q_heads, key_block, preferred_element_type=jnp.float32)
            * scale
        )
        scores = jnp.where(allowed[None], scores, jnp.float32(-1e30))
        new_best = jnp.maximum(best, jnp.max(scores, axis=2))
        factor = jnp.exp(best - new_best)
        expo = jnp.where(allowed[None], jnp.exp(scores - new_best[:, :, None]), jnp.float32(0.0))
        total = total * factor + jnp.sum(expo, axis=2)
        update = jnp.einsum(
            "hqk,khd->qhd",
            expo.astype(jnp.bfloat16),
            value_block,
            preferred_element_type=jnp.float32,
        )
        acc = acc * factor.T[:, :, None] + update
        return (new_best, total, acc)

    best, total, acc = lax.fori_loop(0, count // width, one_block, start_state)
    attended = (acc / total.T[:, :, None]).reshape(rows_ctx, width_heads).astype(jnp.bfloat16)
    attn = lax.psum_scatter(
        jnp.dot(attended, out_weight, preferred_element_type=jnp.float32).astype(jnp.bfloat16),
        "ep",
        scatter_dimension=0,
        tiled=True,
    ).astype(jnp.float32)
    stream = residual.astype(jnp.float32) + attn
    normed = (
        stream * lax.rsqrt(jnp.mean(stream * stream, axis=1, keepdims=True) + 1e-06) * norm_gain
    ).astype(jnp.bfloat16)
    logits = jnp.dot(normed.astype(jnp.float32), router, precision=lax.Precision.HIGHEST)
    gates = jax.nn.sigmoid(jnp.take_along_axis(logits, routes, axis=1))
    weights = gates / jnp.sum(gates, axis=1, keepdims=True)
    experts = router.shape[1]
    top_count = routes.shape[1]
    capacity = min(tok_rows, max(2, 2 * tok_rows * top_count // experts))
    exp_ep = experts // n_ep
    slices = n_ctx // exp_ep
    flat = routes.reshape(-1)
    onehot = (flat[:, None] == jnp.arange(experts, dtype=jnp.int32)[None, :]).astype(jnp.int32)
    rank = jnp.sum((jnp.cumsum(onehot, axis=0) - onehot) * onehot, axis=1)
    slot = (flat * capacity + rank).reshape(tok_rows, top_count)
    placed = slot[:, :, None] == jnp.arange(experts * capacity, dtype=jnp.int32)[None, None, :]
    send_table = jnp.any(placed, axis=1).astype(jnp.bfloat16)
    combine = jnp.sum(jnp.where(placed, weights[:, :, None], jnp.float32(0.0)), axis=1)
    buffer = jnp.einsum("tp,td->pd", send_table, normed, preferred_element_type=jnp.float32).astype(
        jnp.bfloat16
    )
    grid = buffer.reshape(n_ep, exp_ep, capacity, model_width)
    gate_local = gate_weight.reshape(model_width, -1)
    up_local = up_weight.reshape(model_width, -1)
    down_local = down_weight.reshape(-1, model_width)
    owned = lax.all_to_all(grid, "ep", split_axis=0, concat_axis=0, tiled=True)
    copies = jnp.repeat(jnp.swapaxes(owned, 0, 1), slices, axis=0)
    arrived = lax.all_to_all(copies, "ctx", split_axis=0, concat_axis=0, tiled=True)
    rows = arrived.reshape(-1, model_width)
    gate = jnp.dot(rows, gate_local, preferred_element_type=jnp.float32)
    upper = jnp.dot(rows, up_local, preferred_element_type=jnp.float32)
    act = (jax.nn.silu(gate) * upper).astype(jnp.bfloat16)
    partial_value = (
        jnp.dot(act, down_local, preferred_element_type=jnp.float32)
        .astype(jnp.bfloat16)
        .reshape(arrived.shape)
    )
    returned = lax.all_to_all(partial_value, "ctx", split_axis=0, concat_axis=0, tiled=True)
    summed = jnp.sum(
        returned.reshape(exp_ep, slices, n_ep, capacity, model_width).astype(jnp.float32), axis=1
    ).astype(jnp.bfloat16)
    back = lax.all_to_all(jnp.swapaxes(summed, 0, 1), "ep", split_axis=0, concat_axis=0, tiled=True)
    expert_rows = back.reshape(-1, model_width)
    mixed = jnp.dot(combine, expert_rows.astype(jnp.float32), precision=lax.Precision.HIGHEST)
    return (stream + mixed).astype(jnp.bfloat16)


NEG = -1e30
LOG2E = 1.4426950408889634


def attend_kernel(
    where_ref, spans_ref, start_ref, *refs, planes, rows, part, factor
):
    n = planes
    q_in, own_in, oth_in = refs[:n], refs[n : 2 * n], refs[2 * n : 3 * n]
    outs = refs[3 * n : 5 * n]
    q_buf, kv_buf, acc_ref, res_ref, sems = refs[5 * n :]
    z, x, y, core = where_ref[0], where_ref[1], where_ref[2], where_ref[3]
    copies = []
    for s in range(n):
        plane = z ^ s
        copies.append(pltpu.make_async_copy(q_in[s], q_buf.at[s], sems.at[3 * s]))
        copies.append(
            pltpu.make_async_copy(own_in[s], kv_buf.at[2 * plane + x], sems.at[3 * s + 1])
        )
        copies.append(
            pltpu.make_async_copy(oth_in[s], kv_buf.at[2 * plane + 1 - x], sems.at[3 * s + 2])
        )
    for copy in copies:
        copy.start()
    for copy in copies:
        copy.wait()

    for s in range(n):
        block = 2 * (z ^ s) + x
        query = q_buf[s]
        starts = start_ref[pl.ds(block, 1), :]
        q_pos = block * rows + lax.broadcasted_iota(jnp.int32, (1, rows), 1)
        acc_ref[...] = jnp.zeros_like(acc_ref)

        def step(j, state, masked, query=query, starts=starts, q_pos=q_pos):
            best, total = state
            key, value = kv_buf[j, 0], kv_buf[j, 1]
            scores = lax.dot_general(
                key, query, (((1,), (1,)), ((), ())), preferred_element_type=jnp.float32
            )
            if masked:
                k_pos = j * rows + lax.broadcasted_iota(jnp.int32, (rows, rows), 0)
                allowed = (k_pos >= starts) & (k_pos <= q_pos)
                scores = jnp.where(allowed, scores, NEG)
            new_best = jnp.maximum(best, jnp.max(scores, axis=0, keepdims=True))
            expo = jnp.exp2((scores - new_best) * factor)
            shrink = jnp.exp2((best - new_best) * factor)
            total = total * shrink + jnp.sum(expo, axis=0, keepdims=True)
            update = lax.dot_general(
                value,
                expo.astype(jnp.bfloat16),
                (((0,), (0,)), ((), ())),
                preferred_element_type=jnp.float32,
            )
            acc_ref[...] = acc_ref[...] * shrink + update
            return new_best, total

        first = spans_ref[2 * block] // rows
        whole = jnp.minimum((spans_ref[2 * block + 1] + rows - 1) // rows, block)
        state = (jnp.full((1, rows), NEG, jnp.float32), jnp.zeros((1, rows), jnp.float32))
        state = lax.fori_loop(first, whole, functools.partial(step, masked=True), state)
        state = lax.fori_loop(whole, block, functools.partial(step, masked=False), state)
        best, total = step(block, state, True)
        res_ref[...] = jnp.transpose(acc_ref[...] / total)
        for k in range(2):
            for side in range(2):
                row = pl.multiple_of(((y ^ side) * 2 + (core ^ k)) * part, part)
                outs[2 * s + k][pl.ds(side * part, part), :] = res_ref[pl.ds(row, part), :].astype(
                    jnp.bfloat16
                )


def attend(where, spans, starts, q_in, own_in, oth_in):
    planes = len(q_in)
    rows = q_in[0].shape[0]
    part = rows // 4
    any_spec = pl.BlockSpec(memory_space=pl.ANY)
    smem = pl.BlockSpec(memory_space=pltpu.SMEM)
    vmem = pl.BlockSpec(memory_space=pltpu.VMEM)
    return pl.pallas_call(
        functools.partial(
            attend_kernel,
            planes=planes,
            rows=rows,
            part=part,
            factor=HD ** (-0.5) * LOG2E,
        ),
        out_shape=[jax.ShapeDtypeStruct((2 * part, HD), jnp.bfloat16)] * (2 * planes),
        in_specs=[smem, smem, vmem] + [any_spec] * (3 * planes),
        out_specs=[vmem] * (2 * planes),
        scratch_shapes=[
            pltpu.VMEM((planes, rows, HD), jnp.bfloat16),
            pltpu.VMEM((2 * planes, 2, rows, HD), jnp.bfloat16),
            pltpu.VMEM((HD, rows), jnp.float32),
            pltpu.VMEM((rows, HD), jnp.float32),
            pltpu.SemaphoreType.DMA((3 * planes,)),
        ],
        cost_estimate=pl.CostEstimate(
            flops=20 * 4 * rows * rows * HD, bytes_accessed=6 << 20, transcendentals=20 * rows * rows
        ),
        name="attend",
    )(where, spans, starts, *q_in, *own_in, *oth_in)


def dense_body(
    queries,
    keys,
    values,
    segments,
    residual,
    out_weight,
    norm_gain,
    router,
    routes,
    gate_weight,
    up_weight,
    down_weight,
):
    rows = queries.shape[0]
    tok = residual.shape[0]
    n_ctx = lax.axis_size("ctx")
    n_ep = lax.axis_size("ep")
    planes = n_ctx // 2
    ctx, ep = lax.axis_index("ctx"), lax.axis_index("ep")
    z, x, y, core = ctx // 2, ctx % 2, ep // 2, ep % 2
    experts = router.shape[1]
    exp_ep = experts // n_ep
    slices = n_ctx // exp_ep

    def over_x(v):
        return lax.ppermute(v, "ctx", [(c, c ^ 1) for c in range(n_ctx)])

    def over_z(v, s):
        return lax.ppermute(v, "ctx", [(c, c ^ (2 * s)) for c in range(n_ctx)])

    def along_z(v, pairs):
        return lax.ppermute(v, "ctx", [(2 * a + i, 2 * b + i) for a, b in pairs for i in range(2)])

    def over_y(v):
        return lax.ppermute(v, "ep", [(e, e ^ 2) for e in range(n_ep)])

    def over_core(v):
        return lax.ppermute(v, "ep", [(e, e ^ 1) for e in range(n_ep)])

    def over_z_core(v, s, k):
        pairs = [
            (c * n_ep + e, (c ^ (2 * s)) * n_ep + (e ^ k)) for c in range(n_ctx) for e in range(n_ep)
        ]
        return lax.ppermute(v, ("ctx", "ep"), pairs)

    def gather_ep(w):
        far = over_y(w)
        return (w, over_core(w)), (far, over_core(far))

    gate_near, gate_far = gather_ep(gate_weight.reshape(gate_weight.shape[2:]))
    up_near, up_far = gather_ep(up_weight.reshape(up_weight.shape[2:]))
    down_near, down_far = gather_ep(down_weight.reshape(down_weight.shape[2:]))
    gates = [jnp.concatenate(g, axis=1) for g in (gate_near, gate_far)]
    ups = [jnp.concatenate(g, axis=1) for g in (up_near, up_far)]
    downs = [jnp.concatenate(g, axis=0) for g in (down_near, down_far)]

    marks = jnp.any(
        routes[:, :, None] == jnp.arange(experts, dtype=jnp.int32)[None, None, :], axis=1
    ).astype(jnp.float32)
    marks = jnp.stack([marks, over_x(marks)])
    marks = jnp.stack([marks, over_z(marks, 1)])
    marks2 = over_z(marks, 2)
    outer = (z == 0) | (z == planes - 1)
    marks = [
        marks[0],
        marks[1],
        jnp.where(outer, marks2[0], marks2[1]),
        jnp.where(outer, marks2[1], marks2[0]),
    ]
    marks = [m.reshape(2 * tok, experts) for m in marks]

    count = segments.shape[0]
    position = jnp.arange(count, dtype=jnp.int32)
    fresh = jnp.concatenate([jnp.ones((1,), bool), segments[1:] != segments[:-1]])
    starts = lax.cummax(jnp.where(fresh, position, 0)).reshape(n_ctx, rows)
    spans = jnp.stack([starts[:, 0], starts[:, -1]], axis=1).reshape(-1)

    def head(v, s):
        return lax.dynamic_slice_in_dim(v, (z ^ s) * HD, HD, axis=1)

    kv_own = [jnp.stack([head(keys, s), head(values, s)]) for s in range(planes)]
    kv_own = [kv_own[0]] + [over_z(kv_own[s], s) for s in range(1, planes)]
    kv_oth = [over_x(v) for v in kv_own]
    q_in = [head(queries, s) for s in range(planes)]
    q_in = [q_in[0]] + [over_z(q_in[s], s) for s in range(1, planes)]
    outs = attend(jnp.stack([z, x, y, core]), spans, starts, q_in, kv_own, kv_oth)
    pieces = []
    for k in range(2):
        for s in range(planes):
            piece = outs[2 * s + k]
            pieces.append(piece if s == 0 and k == 0 else over_z_core(piece, s, k))
    attended = jnp.concatenate(pieces, axis=1)
    out_heads = out_weight.reshape(planes, HD, -1)
    out_own = jnp.concatenate(
        [lax.dynamic_index_in_dim(out_heads, z ^ s, keepdims=False) for s in range(planes)]
    )
    out_all = jnp.concatenate([out_own, over_core(out_own)])
    far_part = jnp.dot(attended[tok:], out_all, preferred_element_type=jnp.float32)
    far_part = over_y(far_part.astype(jnp.bfloat16))
    near_part = jnp.dot(attended[:tok], out_all, preferred_element_type=jnp.float32)
    stream = residual.astype(jnp.float32) + (near_part + far_part.astype(jnp.float32))
    normed = (
        stream * lax.rsqrt(jnp.mean(stream * stream, axis=1, keepdims=True) + 1e-06) * norm_gain
    ).astype(jnp.bfloat16)

    inner = [(1, 2), (2, 1)]
    outward = [(1, 0), (2, 3)]
    inward = [(0, 1), (3, 2)]
    tok1 = over_z(normed, 1)
    tok2 = along_z(normed, inner)
    tok3 = along_z(tok1, inner)
    tok2 = tok2 + along_z(tok2, outward)
    tok3 = tok3 + along_z(tok3, outward)
    own = [normed, tok1, tok2, tok3]
    both = [jnp.concatenate([v, over_x(v)]) for v in own]

    parts = []
    left = router
    for _ in range(3):
        cut = lax.reduce_precision(left, 8, 7)
        parts.append(cut.astype(jnp.bfloat16))
        left = left - cut
    router_parts = jnp.concatenate(parts, axis=1)
    half = gate_weight.shape[3]
    which = [ep, ep ^ 1, ep ^ 2, ep ^ 3]
    which = [w * exp_ep + ctx // slices for w in which]

    def run_experts(tokens, mark):
        logits = jnp.dot(tokens, router_parts, preferred_element_type=jnp.float32)
        logits = logits[:, :experts] + logits[:, experts : 2 * experts] + logits[:, 2 * experts :]
        gate = jax.nn.sigmoid(logits) * mark
        weights = gate / jnp.sum(gate, axis=1, keepdims=True)
        column = lax.broadcasted_iota(jnp.int32, (1, experts), 1)
        picked = [
            jnp.sum(jnp.where(column == w, weights, 0.0), axis=1, keepdims=True) for w in which
        ]
        total = None
        for group in range(2):
            a = jnp.dot(tokens, gates[group], preferred_element_type=jnp.float32)
            b = jnp.dot(tokens, ups[group], preferred_element_type=jnp.float32)
            lane = lax.broadcasted_iota(jnp.int32, (1, 2 * half), 1)
            scale = jnp.where(lane < half, picked[2 * group], picked[2 * group + 1])
            act = (jax.nn.silu(a) * b * scale).astype(jnp.bfloat16)
            term = jnp.dot(act, downs[group], preferred_element_type=jnp.float32)
            total = term if total is None else total + term
        return total

    near = run_experts(jnp.concatenate(both[:2]), jnp.concatenate(marks[:2]))
    far = run_experts(jnp.concatenate(both[2:]), jnp.concatenate(marks[2:]))
    chunks = [near[: 2 * tok], near[2 * tok :], far[: 2 * tok], far[2 * tok :]]

    def send(v):
        return v.astype(jnp.bfloat16)

    sums = [None] * 4
    for k in (3, 2, 1, 0):
        sums[k] = chunks[k][:tok] + over_x(send(chunks[k][tok:])).astype(jnp.float32)
    got = along_z(send(sums[3]), inward).astype(jnp.float32)
    got = along_z(send(sums[3] + got), inner).astype(jnp.float32)
    mid = along_z(send(sums[2]), inward).astype(jnp.float32)
    mid = along_z(send(sums[2] + mid), inner).astype(jnp.float32)
    last = over_z(send(sums[1] + got), 1).astype(jnp.float32)
    return (stream + (sums[0] + mid + last)).astype(jnp.bfloat16)


def body(*arrays):
    queries, residual, router, routes = arrays[0], arrays[4], arrays[7], arrays[8]
    n_ctx, n_ep = lax.axis_size("ctx"), lax.axis_size("ep")
    rows_all = residual.shape[0] * routes.shape[1]
    dense = 4 * rows_all >= 3 * residual.shape[0] * router.shape[1]
    shaped = n_ctx == 8 and n_ep == 4 and queries.shape[1] == n_ctx // 2 * HD
    if dense and shaped:
        return dense_body(*arrays)
    return general_body(*arrays)


def solution(mesh):
    placed = (
        P("ctx", "ep"),
        P("ctx", "ep"),
        P("ctx", "ep"),
        P(),
        P(("ctx", "ep"), None),
        P("ep", None),
        P(),
        P(),
        P(("ctx", "ep"), None),
        P("ep", "ctx", None, None),
        P("ep", "ctx", None, None),
        P("ep", "ctx", None, None),
    )
    return jax.shard_map(
        body, mesh=mesh, in_specs=placed, out_specs=P(("ctx", "ep"), None), check_vma=False
    )
```

```python
import functools

import jax
import jax.numpy as jnp
from jax import lax
from jax.experimental import pallas as pl
from jax.experimental.pallas import tpu as pltpu
from jax.sharding import PartitionSpec as P


HD = 128


def general_body(
    queries,
    keys,
    values,
    segments,
    residual,
    out_weight,
    norm_gain,
    router,
    routes,
    gate_weight,
    up_weight,
    down_weight,
):
    rows_ctx = queries.shape[0]
    width_heads = queries.shape[1]
    heads_dev = width_heads // HD
    model_width = residual.shape[1]
    tok_rows = residual.shape[0]
    n_ctx = lax.axis_size("ctx")
    n_ep = lax.axis_size("ep")
    first = lax.axis_index("ctx") * rows_ctx
    q_pos = first + jnp.arange(rows_ctx, dtype=jnp.int32)
    q_seg = lax.dynamic_slice_in_dim(segments, first, rows_ctx)
    q_heads = queries.reshape(rows_ctx, heads_dev, HD)
    scale = HD ** (-0.5)
    start_state = (
        jnp.full((heads_dev, rows_ctx), -1e30, jnp.float32),
        jnp.zeros((heads_dev, rows_ctx), jnp.float32),
        jnp.zeros((rows_ctx, heads_dev, HD), jnp.float32),
    )
    key_rows = lax.all_gather(keys, "ctx", axis=0, tiled=True)
    value_rows = lax.all_gather(values, "ctx", axis=0, tiled=True)
    count = key_rows.shape[0]
    width = 512

    def one_block(step, state):
        best, total, acc = state
        offset = step * width
        key_block = lax.dynamic_slice_in_dim(key_rows, offset, width).reshape(width, heads_dev, HD)
        value_block = lax.dynamic_slice_in_dim(value_rows, offset, width).reshape(
            width, heads_dev, HD
        )
        k_pos = offset + jnp.arange(width, dtype=jnp.int32)
        k_seg = lax.dynamic_slice_in_dim(segments, offset, width)
        allowed = (q_seg[:, None] == k_seg[None, :]) & (k_pos[None, :] <= q_pos[:, None])
        scores = (
            jnp.einsum("qhd,khd->hqk", q_heads, key_block, preferred_element_type=jnp.float32)
            * scale
        )
        scores = jnp.where(allowed[None], scores, jnp.float32(-1e30))
        new_best = jnp.maximum(best, jnp.max(scores, axis=2))
        factor = jnp.exp(best - new_best)
        expo = jnp.where(allowed[None], jnp.exp(scores - new_best[:, :, None]), jnp.float32(0.0))
        total = total * factor + jnp.sum(expo, axis=2)
        update = jnp.einsum(
            "hqk,khd->qhd",
            expo.astype(jnp.bfloat16),
            value_block,
            preferred_element_type=jnp.float32,
        )
        acc = acc * factor.T[:, :, None] + update
        return (new_best, total, acc)

    _, total, acc = lax.fori_loop(0, count // width, one_block, start_state)
    attended = (acc / total.T[:, :, None]).reshape(rows_ctx, width_heads).astype(jnp.bfloat16)
    attn = lax.psum_scatter(
        jnp.dot(attended, out_weight, preferred_element_type=jnp.float32).astype(jnp.bfloat16),
        "ep",
        scatter_dimension=0,
        tiled=True,
    ).astype(jnp.float32)
    stream = residual.astype(jnp.float32) + attn
    normed = (
        stream * lax.rsqrt(jnp.mean(stream * stream, axis=1, keepdims=True) + 1e-06) * norm_gain
    ).astype(jnp.bfloat16)
    logits = jnp.dot(normed.astype(jnp.float32), router, precision=lax.Precision.HIGHEST)
    gates = jax.nn.sigmoid(jnp.take_along_axis(logits, routes, axis=1))
    weights = gates / jnp.sum(gates, axis=1, keepdims=True)
    experts = router.shape[1]
    top_count = routes.shape[1]
    capacity = min(tok_rows, max(2, 2 * tok_rows * top_count // experts))
    exp_ep = experts // n_ep
    slices = n_ctx // exp_ep
    flat = routes.reshape(-1)
    onehot = (flat[:, None] == jnp.arange(experts, dtype=jnp.int32)[None, :]).astype(jnp.int32)
    rank = jnp.sum((jnp.cumsum(onehot, axis=0) - onehot) * onehot, axis=1)
    slot = (flat * capacity + rank).reshape(tok_rows, top_count)
    placed = slot[:, :, None] == jnp.arange(experts * capacity, dtype=jnp.int32)[None, None, :]
    send_table = jnp.any(placed, axis=1).astype(jnp.bfloat16)
    combine = jnp.sum(jnp.where(placed, weights[:, :, None], jnp.float32(0.0)), axis=1)
    buffer = jnp.einsum("tp,td->pd", send_table, normed, preferred_element_type=jnp.float32).astype(
        jnp.bfloat16
    )
    grid = buffer.reshape(n_ep, exp_ep, capacity, model_width)
    gate_local = gate_weight.reshape(model_width, -1)
    up_local = up_weight.reshape(model_width, -1)
    down_local = down_weight.reshape(-1, model_width)
    owned = lax.all_to_all(grid, "ep", split_axis=0, concat_axis=0, tiled=True)
    copies = jnp.repeat(jnp.swapaxes(owned, 0, 1), slices, axis=0)
    arrived = lax.all_to_all(copies, "ctx", split_axis=0, concat_axis=0, tiled=True)
    rows = arrived.reshape(-1, model_width)
    gate = jnp.dot(rows, gate_local, preferred_element_type=jnp.float32)
    upper = jnp.dot(rows, up_local, preferred_element_type=jnp.float32)
    act = (jax.nn.silu(gate) * upper).astype(jnp.bfloat16)
    partial_value = (
        jnp.dot(act, down_local, preferred_element_type=jnp.float32)
        .astype(jnp.bfloat16)
        .reshape(arrived.shape)
    )
    returned = lax.all_to_all(partial_value, "ctx", split_axis=0, concat_axis=0, tiled=True)
    summed = jnp.sum(
        returned.reshape(exp_ep, slices, n_ep, capacity, model_width).astype(jnp.float32), axis=1
    ).astype(jnp.bfloat16)
    back = lax.all_to_all(jnp.swapaxes(summed, 0, 1), "ep", split_axis=0, concat_axis=0, tiled=True)
    expert_rows = back.reshape(-1, model_width)
    mixed = jnp.dot(combine, expert_rows.astype(jnp.float32), precision=lax.Precision.HIGHEST)
    return (stream + mixed).astype(jnp.bfloat16)


NEG = -1e30
LOG2E = 1.4426950408889634
STREAMS = 2


def attend_kernel(where_ref, ids_ref, seg_ref, *refs, planes, rows, part, factor, own):
    n = planes
    q_in, kv_in, refs = refs[:n], refs[n : 2 * n], refs[2 * n :]
    if own:
        acc_ref, stat_ref, q_buf, kv_buf, col_ref, sems = refs
    else:
        acc_in, stat_in, *outs, acc_ref, stat_ref, res_ref, q_buf, kv_buf, col_ref, sems = refs
    z, x, y, core = where_ref[0], where_ref[1], where_ref[2], where_ref[3]
    side = x if own else 1 - x
    copies = []
    for s in range(n):
        copies.append(pltpu.make_async_copy(q_in[s], q_buf.at[s], sems.at[2 * s]))
        copies.append(pltpu.make_async_copy(kv_in[s], kv_buf.at[z ^ s], sems.at[2 * s + 1]))
    for copy in copies:
        copy.start()
    turned = jnp.transpose(seg_ref[...])
    for j in range(2 * n):
        col_ref[j] = turned[:, j : j + 1]
    if own:
        acc_ref[...] = jnp.zeros_like(acc_ref)
    else:
        acc_ref[...] = acc_in[...]
        stat_ref[...] = stat_in[...]
    for copy in copies:
        copy.wait()

    def one_slot(s, carry):
        plane = z ^ s
        block = 2 * plane + x
        query = q_buf[s]
        q_seg = seg_ref[pl.ds(block, 1), :]
        q_pos = block * rows + lax.broadcasted_iota(jnp.int32, (1, rows), 1)

        def step(p, state, masked):
            best, total = state
            key, value = kv_buf[p, 0], kv_buf[p, 1]
            scores = lax.dot_general(
                key, query, (((1,), (1,)), ((), ())), preferred_element_type=jnp.float32
            )
            if masked:
                j = 2 * p + side
                allowed = col_ref[j] == q_seg
                if own:
                    k_pos = j * rows + lax.broadcasted_iota(jnp.int32, (rows, rows), 0)
                    allowed = allowed & (k_pos <= q_pos)
                scores = jnp.where(allowed, scores, NEG)
            new_best = jnp.maximum(best, jnp.max(scores, axis=0, keepdims=True))
            expo = jnp.exp2((scores - new_best) * factor)
            shrink = jnp.exp2((best - new_best) * factor)
            total = total * shrink + jnp.sum(expo, axis=0, keepdims=True)
            update = lax.dot_general(
                value,
                expo.astype(jnp.bfloat16),
                (((0,), (0,)), ((), ())),
                preferred_element_type=jnp.float32,
            )
            acc_ref[s] = acc_ref[s] * shrink + update
            return new_best, total

        low, high = ids_ref[block * rows], ids_ref[block * rows + rows - 1]
        last = plane if own else plane + x
        first, whole = jnp.int32(0), jnp.int32(0)
        for p in range(n):
            start = (2 * p + side) * rows
            first += (ids_ref[start + rows - 1] < low).astype(jnp.int32)
            whole += (ids_ref[start] < high).astype(jnp.int32)
        first, whole = jnp.minimum(first, last), jnp.minimum(whole, last)
        if own:
            state = (jnp.full((1, rows), NEG, jnp.float32), jnp.zeros((1, rows), jnp.float32))
        else:
            stats = stat_ref[s]
            state = (stats[0:1], stats[1:2])
        state = lax.fori_loop(first, whole, functools.partial(step, masked=True), state)
        state = lax.fori_loop(whole, last, functools.partial(step, masked=False), state)
        if own:
            best, total = step(plane, state, True)
            stat_ref[s, 0:1] = best
            stat_ref[s, 1:2] = total
        else:
            res_ref[s] = jnp.transpose(acc_ref[s] / state[1])
        return carry

    lax.fori_loop(0, n, one_slot, 0)
    if own:
        return
    for s in range(n):
        for k in range(2):
            for half in range(2):
                row = pl.multiple_of(((y ^ half) * 2 + (core ^ k)) * part, part)
                outs[2 * s + k][pl.ds(half * part, part), :] = res_ref[
                    s, pl.ds(row, part), :
                ].astype(jnp.bfloat16)


def attend(where, segments, q_in, kv_in, state):
    planes = len(q_in)
    rows = q_in[0].shape[0]
    part = rows // 4
    own = state is None
    any_spec = pl.BlockSpec(memory_space=pl.ANY)
    smem = pl.BlockSpec(memory_space=pltpu.SMEM)
    vmem = pl.BlockSpec(memory_space=pltpu.VMEM)
    kept = [(planes, HD, rows), (planes, 8, rows)]
    if own:
        shapes, states = [jax.ShapeDtypeStruct(k, jnp.float32) for k in kept], []
    else:
        shapes = [jax.ShapeDtypeStruct((2 * part, HD), jnp.bfloat16)] * (2 * planes)
        states = [pltpu.VMEM(k, jnp.float32) for k in kept]
        states.append(pltpu.VMEM((planes, rows, HD), jnp.float32))
    return pl.pallas_call(
        functools.partial(
            attend_kernel,
            planes=planes,
            rows=rows,
            part=part,
            factor=HD ** (-0.5) * LOG2E,
            own=own,
        ),
        out_shape=shapes,
        in_specs=[smem, smem, vmem] + [any_spec] * (2 * planes) + [vmem] * (0 if own else 2),
        out_specs=[vmem] * len(shapes),
        scratch_shapes=states
        + [
            pltpu.VMEM((planes, rows, HD), jnp.bfloat16),
            pltpu.VMEM((planes, 2, rows, HD), jnp.bfloat16),
            pltpu.VMEM((2 * planes, rows, 1), jnp.float32),
            pltpu.SemaphoreType.DMA((2 * planes,)),
        ],
        compiler_params=pltpu.CompilerParams(vmem_limit_bytes=24 << 20),
        cost_estimate=pl.CostEstimate(
            flops=10 * 4 * rows * rows * HD, bytes_accessed=4 << 20, transcendentals=10 * rows * rows
        ),
        name="attend_own" if own else "attend_other",
    )(
        where,
        segments,
        segments.astype(jnp.float32).reshape(2 * planes, rows),
        *q_in,
        *kv_in,
        *([] if own else state),
    )


def split_kernel(where_ref, q_ref, k_ref, v_ref, *outs):
    planes = len(outs) // 2
    for s in reversed(range(planes)):
        lanes = pl.ds(pl.multiple_of((where_ref[0] ^ s) * HD, HD), HD)
        outs[planes + s][0] = k_ref[:, lanes]
        outs[planes + s][1] = v_ref[:, lanes]
        outs[s][...] = q_ref[:, lanes]


def split_heads(where, queries, keys, values):
    rows, width = queries.shape
    planes = width // HD
    vmem = pl.BlockSpec(memory_space=pltpu.VMEM)
    outs = pl.pallas_call(
        split_kernel,
        out_shape=[jax.ShapeDtypeStruct((rows, HD), jnp.bfloat16)] * planes
        + [jax.ShapeDtypeStruct((2, rows, HD), jnp.bfloat16)] * planes,
        in_specs=[pl.BlockSpec(memory_space=pltpu.SMEM)] + [vmem] * 3,
        out_specs=[vmem] * (2 * planes),
        cost_estimate=pl.CostEstimate(
            flops=0, bytes_accessed=12 * rows * width, transcendentals=0
        ),
        name="split_heads",
    )(where, queries, keys, values)
    return outs[:planes], outs[planes:]


def far_kernel(where_ref, *refs, planes):
    pieces, (own_weight, oth_weight, *far, near_out, wide) = refs[: 2 * planes], refs[2 * planes :]
    tok = near_out.shape[0]
    deep = planes * HD
    for k in range(2):
        for s in range(planes):
            piece = pieces[k * planes + s]
            lanes = pl.ds(pl.multiple_of(k * deep + (where_ref[0] ^ s) * HD, HD), HD)
            wide[:, lanes] = piece[tok:]
            near_out[:, lanes] = piece[:tok]
    total = (
        jnp.dot(wide[:, :deep], own_weight[...], preferred_element_type=jnp.float32)
        + jnp.dot(wide[:, deep:], oth_weight[...], preferred_element_type=jnp.float32)
    ).astype(jnp.bfloat16)
    part = tok // len(far)
    for i, out in enumerate(far):
        out[...] = total[i * part : (i + 1) * part]


def project_far(where, pieces, own_weight, oth_weight):
    tok = pieces[0].shape[0] // 2
    deep, wide = own_weight.shape
    vmem = pl.BlockSpec(memory_space=pltpu.VMEM)
    return pl.pallas_call(
        functools.partial(far_kernel, planes=len(pieces) // 2),
        out_shape=[
            jax.ShapeDtypeStruct((tok // STREAMS, wide), jnp.bfloat16),
        ]
        * STREAMS
        + [jax.ShapeDtypeStruct((tok, 2 * deep), jnp.bfloat16)],
        in_specs=[pl.BlockSpec(memory_space=pltpu.SMEM)] + [vmem] * (len(pieces) + 2),
        out_specs=[vmem] * (STREAMS + 1),
        scratch_shapes=[pltpu.VMEM((tok, 2 * deep), jnp.bfloat16)],
        cost_estimate=pl.CostEstimate(
            flops=4 * tok * deep * wide, bytes_accessed=4 * deep * wide, transcendentals=0
        ),
        compiler_params=pltpu.CompilerParams(vmem_limit_bytes=24 << 20),
        name="project_far",
    )(where, *pieces, own_weight, oth_weight)


def near_kernel(attended, own_weight, oth_weight, residual, *outs):
    deep = own_weight.shape[0]
    total = residual[...].astype(jnp.float32) + (
        jnp.dot(attended[:, :deep], own_weight[...], preferred_element_type=jnp.float32)
        + jnp.dot(attended[:, deep:], oth_weight[...], preferred_element_type=jnp.float32)
    )
    part = total.shape[0] // len(outs)
    for i, out in enumerate(outs):
        out[...] = total[i * part : (i + 1) * part]


def project_near(attended, own_weight, oth_weight, residual):
    deep, wide = own_weight.shape
    vmem = pl.BlockSpec(memory_space=pltpu.VMEM)
    return pl.pallas_call(
        near_kernel,
        out_shape=[
            jax.ShapeDtypeStruct((residual.shape[0] // STREAMS, wide), jnp.float32)
        ]
        * STREAMS,
        in_specs=[vmem] * 4,
        out_specs=[vmem] * STREAMS,
        cost_estimate=pl.CostEstimate(
            flops=4 * attended.shape[0] * deep * wide,
            bytes_accessed=4 * deep * wide,
            transcendentals=0,
        ),
        compiler_params=pltpu.CompilerParams(vmem_limit_bytes=24 << 20),
        name="project_near",
    )(attended, own_weight, oth_weight, residual)


def norm_kernel(near, far, gain, stream_out, normed_out):
    stream = near[...] + far[...].astype(jnp.float32)
    stream_out[...] = stream
    mean = jnp.mean(stream * stream, axis=1, keepdims=True)
    normed_out[...] = (stream * lax.rsqrt(mean + 1e-06) * gain[...]).astype(jnp.bfloat16)


def add_norm(near, far, gain):
    vmem = pl.BlockSpec(memory_space=pltpu.VMEM)
    return pl.pallas_call(
        norm_kernel,
        out_shape=[
            jax.ShapeDtypeStruct(near.shape, jnp.float32),
            jax.ShapeDtypeStruct(near.shape, jnp.bfloat16),
        ],
        in_specs=[vmem] * 3,
        out_specs=[vmem] * 2,
        cost_estimate=pl.CostEstimate(
            flops=4 * near.size, bytes_accessed=12 * near.size, transcendentals=near.shape[0]
        ),
        compiler_params=pltpu.CompilerParams(vmem_limit_bytes=24 << 20),
        name="add_norm",
    )(near, far, gain.reshape(1, -1))


def project_down(act_ref, first, down_buf, copies, outs):
    tok, wide = outs[0].shape
    step = wide // len(copies)
    for n, group in enumerate(copies):
        for copy in group:
            copy.wait()
        cols = slice(n * step, (n + 1) * step)
        part = jnp.dot(
            act_ref[first : first + len(outs) * tok, :],
            down_buf[:, cols],
            preferred_element_type=jnp.float32,
        )
        for i, out in enumerate(outs):
            out[:, cols] = part[i * tok : (i + 1) * tok].astype(out.dtype)


def down_shapes(tok, wide, pieces):
    return [jax.ShapeDtypeStruct((tok, wide), jnp.float32)] * (pieces // 2) + [
        jax.ShapeDtypeStruct((tok, wide), jnp.bfloat16)
    ] * (pieces // 2)


def experts_kernel(which_ref, *refs, pieces, slots, experts, half):
    tokens, refs = refs[:pieces], refs[pieces:]
    marks, router_ref, refs = refs[:slots], refs[slots], refs[slots + 1 :]
    weights, refs = refs[:8], refs[8:]
    act_out, outs, refs = refs[0], refs[1 : 1 + pieces // 2], refs[1 + pieces // 2 :]
    rows_ref, up_buf, down_buf, act_ref, pick_ref, sems = refs
    tok = tokens[0].shape[0]
    loads = [
        pltpu.make_async_copy(tokens[i], rows_ref.at[pl.ds(i * tok, tok), :], sems.at[9 + i])
        for i in range(pieces)
    ]
    ups = [pltpu.make_async_copy(weights[2 * i], up_buf.at[i], sems.at[2 * i]) for i in range(4)]
    downs = [
        pltpu.make_async_copy(
            weights[2 * i + 1], down_buf.at[pl.ds(i * half, half), :], sems.at[2 * i + 1]
        )
        for i in range(4)
    ]
    for copy in loads + ups[:2]:
        copy.start()
    for copy in loads:
        copy.wait()
    logits = lax.dot_general(
        router_ref[...],
        rows_ref[...],
        (((1,), (1,)), ((), ())),
        preferred_element_type=jnp.float32,
    )
    logits = logits[:experts] + logits[experts : 2 * experts] + logits[2 * experts :]
    group = slots // 2
    mark = jnp.concatenate(
        [
            m[i * experts : (i + 1) * experts, :]
            for first in (0, group)
            for i in range(2)
            for m in marks[first : first + group]
        ],
        axis=1,
    )
    gate = mark / (1.0 + jnp.exp(-logits))
    weight = gate / jnp.sum(gate, axis=0, keepdims=True)
    row = lax.broadcasted_iota(jnp.int32, weight.shape, 0)
    picked = [
        jnp.sum(jnp.where(row == which_ref[i], weight, 0.0), axis=0, keepdims=True)
        for i in range(4)
    ]
    pick_ref[...] = jnp.transpose(jnp.concatenate(picked + picked, axis=0))
    rows = pieces * tok
    for i in range(4):
        ups[i].wait()
        for copy in ups[i + 2 : i + 3] if i < 2 else downs[2 * i - 4 : 2 * i - 2]:
            copy.start()
        for first in range(0, rows, rows // 2):
            block = slice(first, first + rows // 2)
            a = lax.dot_general(
                rows_ref[block, :],
                up_buf[i],
                (((1,), (1,)), ((), ())),
                preferred_element_type=jnp.float32,
            )
            a, b = a[:, :half], a[:, half:]
            act_ref[block, i * half : (i + 1) * half] = (
                a / (1.0 + jnp.exp(-a)) * b * pick_ref[block, i : i + 1]
            ).astype(jnp.bfloat16)
    store = pltpu.make_async_copy(act_ref.at[pl.ds(0, rows // 2), :], act_out, sems.at[8])
    store.start()
    project_down(act_ref, rows // 2, down_buf, [downs, [], [], []], outs)
    store.wait()


def run_experts(which, tokens, marks, router_parts, weights, experts):
    pieces = len(tokens)
    tok, wide = tokens[0].shape
    half = weights[1].shape[0]
    rows = pieces * tok
    vmem = pl.BlockSpec(memory_space=pltpu.VMEM)
    anywhere = pl.BlockSpec(memory_space=pl.ANY)
    act, *outs = pl.pallas_call(
        functools.partial(
            experts_kernel, pieces=pieces, slots=len(marks), experts=experts, half=half
        ),
        out_shape=[jax.ShapeDtypeStruct((rows // 2, 4 * half), jnp.bfloat16)]
        + down_shapes(tok, wide, pieces // 2),
        in_specs=[pl.BlockSpec(memory_space=pltpu.SMEM)]
        + [anywhere] * pieces
        + [vmem] * (len(marks) + 1)
        + [anywhere] * 8,
        out_specs=[anywhere] + [vmem] * (pieces // 2),
        scratch_shapes=[
            pltpu.VMEM((rows, wide), jnp.bfloat16),
            pltpu.VMEM((4, 2 * half, wide), jnp.bfloat16),
            pltpu.VMEM((4 * half, wide), jnp.bfloat16),
            pltpu.VMEM((rows, 4 * half), jnp.bfloat16),
            pltpu.VMEM((rows, 8), jnp.float32),
            pltpu.SemaphoreType.DMA((9 + pieces,)),
        ],
        cost_estimate=pl.CostEstimate(
            flops=5 * rows * wide * half * 4,
            bytes_accessed=6 * wide * half * 4,
            transcendentals=rows * half * 4,
        ),
        name="experts",
    )(which, *tokens, *marks, router_parts, *weights)
    return act, outs


def down_kernel(act_ref, *refs, half):
    weights, outs, (down_buf, sems) = refs[:4], refs[4:-2], refs[-2:]
    step = down_buf.shape[1] // 4
    copies = [
        [
            pltpu.make_async_copy(
                weights[i].at[:, pl.ds(n * step, step)],
                down_buf.at[pl.ds(i * half, half), pl.ds(n * step, step)],
                sems.at[4 * n + i],
            )
            for i in range(4)
        ]
        for n in range(4)
    ]
    for group in copies:
        for copy in group:
            copy.start()
    project_down(act_ref, 0, down_buf, copies, outs)


def finish_experts(act, weights, pieces):
    rows = act.shape[0]
    half, wide = weights[0].shape
    return pl.pallas_call(
        functools.partial(down_kernel, half=half),
        out_shape=down_shapes(rows // pieces, wide, pieces),
        in_specs=[pl.BlockSpec(memory_space=pltpu.VMEM)] + [pl.BlockSpec(memory_space=pl.ANY)] * 4,
        out_specs=[pl.BlockSpec(memory_space=pltpu.VMEM)] * pieces,
        scratch_shapes=[
            pltpu.VMEM((4 * half, wide), jnp.bfloat16),
            pltpu.SemaphoreType.DMA((16,)),
        ],
        cost_estimate=pl.CostEstimate(
            flops=2 * rows * wide * half * 4,
            bytes_accessed=2 * wide * half * 4,
            transcendentals=0,
        ),
        name="finish_experts",
    )(act, *weights)


def dense_body(
    queries,
    keys,
    values,
    segments,
    residual,
    out_weight,
    norm_gain,
    router,
    routes,
    gate_weight,
    up_weight,
    down_weight,
):
    n_ctx = lax.axis_size("ctx")
    n_ep = lax.axis_size("ep")
    planes = n_ctx // 2
    ctx, ep = lax.axis_index("ctx"), lax.axis_index("ep")
    z, x, y, core = ctx // 2, ctx % 2, ep // 2, ep % 2
    experts = router.shape[1]
    exp_ep = experts // n_ep
    slices = n_ctx // exp_ep

    def over_x(v):
        return lax.ppermute(v, "ctx", [(c, c ^ 1) for c in range(n_ctx)])

    def over_z(v, s):
        return lax.ppermute(v, "ctx", [(c, c ^ (2 * s)) for c in range(n_ctx)])

    def along_z(v, pairs):
        return lax.ppermute(v, "ctx", [(2 * a + i, 2 * b + i) for a, b in pairs for i in range(2)])

    def over_y(v):
        return lax.ppermute(v, "ep", [(e, e ^ 2) for e in range(n_ep)])

    def over_core(v):
        return lax.ppermute(v, "ep", [(e, e ^ 1) for e in range(n_ep)])

    def over_z_core(v, s, k):
        pairs = [
            (c * n_ep + e, (c ^ (2 * s)) * n_ep + (e ^ k)) for c in range(n_ctx) for e in range(n_ep)
        ]
        return lax.ppermute(v, ("ctx", "ep"), pairs)

    where = jnp.stack([z, x, y, core])

    q_send, kv_send = split_heads(where, queries, keys, values)
    kv_own, q_in = [None] * planes, [None] * planes
    for s in reversed(range(planes)):
        kv_own[s] = over_z(kv_send[s], s) if s else kv_send[s]
    for s in reversed(range(planes)):
        q_in[s] = over_z(q_send[s], s) if s else q_send[s]
    kv_oth = []
    for s in range(planes):
        kv_oth.append(over_x(kv_own[s]))

    def gather_ep(w):
        far = over_y(w)
        near_other = over_core(w)
        far_other = over_core(far)
        return [w, near_other, far, far_other]

    def rows_first(w):
        return jnp.swapaxes(w.reshape(w.shape[2:]), 0, 1)

    up_all = gather_ep(jnp.concatenate([rows_first(gate_weight), rows_first(up_weight)]))
    down_all = gather_ep(down_weight.reshape(down_weight.shape[2:]))
    weights = [w for pair in zip(up_all, down_all) for w in pair]
    out_oth = over_core(out_weight)

    expert_ids = jnp.arange(experts, dtype=jnp.int32)
    mark = jnp.any(routes.T[:, None, :] == expert_ids[None, :, None], axis=0).astype(jnp.float32)
    mark = jnp.concatenate([mark, over_x(mark)])
    marks = [mark]
    for s in range(1, planes):
        marks.append(over_z(mark, s))
    outer = (z == 0) | (z == planes - 1)
    marks[2:] = [jnp.where(outer, marks[2], marks[3]), jnp.where(outer, marks[3], marks[2])]

    state = attend(where, segments, q_in, kv_own, None)
    outs = attend(where, segments, q_in, kv_oth, state)
    pieces = []
    for k in range(2):
        for s in range(planes):
            piece = outs[2 * s + k]
            pieces.append(piece if s == 0 and k == 0 else over_z_core(piece, s, k))
    *far_parts, attended = project_far(where, pieces, out_weight, out_oth)
    far = []
    for h in range(STREAMS):
        far.append(over_y(far_parts[h]))
    near = project_near(attended, out_weight, out_oth, residual)

    inner = [(1, 2), (2, 1)]
    stream, own, oth = [], [], []
    for h in range(STREAMS):
        kept, normed = add_norm(near[h], far[h], norm_gain)
        stream.append(kept)
        tok1 = over_z(normed, 1)
        tok2 = along_z(normed, inner)
        tok3 = along_z(tok1, inner)
        tok2 = jnp.where(outer, over_z(tok2, 1), tok2)
        tok3 = jnp.where(outer, over_z(tok3, 1), tok3)
        own.append((normed, tok1, tok2, tok3))
        others = []
        for k in range(4):
            others.append(over_x(own[h][k]))
        oth.append(others)

    parts = []
    left = router
    for _ in range(3):
        cut = lax.reduce_precision(left, 8, 7)
        parts.append(cut.astype(jnp.bfloat16))
        left = left - cut
    router_parts = jnp.concatenate([part.T for part in parts])
    which = jnp.stack([w * exp_ep + ctx // slices for w in (ep, ep ^ 1, ep ^ 2, ep ^ 3)])

    def of_slots(pair, sides=(own, oth)):
        return [side[h][k] for side in sides for k in pair for h in range(STREAMS)]

    keep, back = [None] * 4, [None] * 4

    def deal(pair, outs):
        for i, k in enumerate(pair):
            keep[k] = outs[i * STREAMS : (i + 1) * STREAMS]
            back[k] = outs[(2 + i) * STREAMS : (3 + i) * STREAMS]

    near_slots, far_slots = (0, 1), (2, 3)
    act, outs = run_experts(
        which, of_slots(near_slots) + of_slots(far_slots), marks, router_parts, weights, experts
    )
    deal(far_slots, outs)
    deal(near_slots, finish_experts(act, down_all, 4 * STREAMS))

    def wide(v):
        return v.astype(jnp.float32)

    def send(v):
        return v.astype(jnp.bfloat16)

    def from_outer(v):
        return jnp.where(outer, 0.0, wide(over_z(send(v), 1)))

    result = []
    for h in range(STREAMS):
        sums = [None] * 4
        for k in (3, 2, 1, 0):
            sums[k] = keep[k][h] + wide(over_x(back[k][h]))
        got = from_outer(sums[3])
        got = wide(along_z(send(sums[3] + got), inner))
        mid = from_outer(sums[2])
        mid = wide(along_z(send(sums[2] + mid), inner))
        last = wide(over_z(send(sums[1] + got), 1))
        result.append(send(stream[h] + (sums[0] + mid + last)))
    return jnp.concatenate(result)


def body(*arrays):
    queries, residual, router, routes = arrays[0], arrays[4], arrays[7], arrays[8]
    n_ctx, n_ep = lax.axis_size("ctx"), lax.axis_size("ep")
    rows_all = residual.shape[0] * routes.shape[1]
    dense = 4 * rows_all >= 3 * residual.shape[0] * router.shape[1]
    shaped = n_ctx == 8 and n_ep == 4 and queries.shape[1] == n_ctx // 2 * HD
    if dense and shaped:
        return dense_body(*arrays)
    return general_body(*arrays)


def solution(mesh):
    placed = (
        P("ctx", "ep"),
        P("ctx", "ep"),
        P("ctx", "ep"),
        P(),
        P(("ctx", "ep"), None),
        P("ep", None),
        P(),
        P(),
        P(("ctx", "ep"), None),
        P("ep", "ctx", None, None),
        P("ep", "ctx", None, None),
        P("ep", "ctx", None, None),
    )
    return jax.shard_map(
        body, mesh=mesh, in_specs=placed, out_specs=P(("ctx", "ep"), None), check_vma=False
    )
```

```python
import functools

import jax
import jax.numpy as jnp
from jax import lax
from jax.experimental import pallas as pl
from jax.experimental.pallas import tpu as pltpu
from jax.sharding import PartitionSpec as P


HD = 128


def general_body(
    queries,
    keys,
    values,
    segments,
    residual,
    out_weight,
    norm_gain,
    router,
    routes,
    gate_weight,
    up_weight,
    down_weight,
):
    rows_ctx = queries.shape[0]
    width_heads = queries.shape[1]
    heads_dev = width_heads // HD
    model_width = residual.shape[1]
    tok_rows = residual.shape[0]
    n_ctx = lax.axis_size("ctx")
    n_ep = lax.axis_size("ep")
    first = lax.axis_index("ctx") * rows_ctx
    q_pos = first + jnp.arange(rows_ctx, dtype=jnp.int32)
    q_seg = lax.dynamic_slice_in_dim(segments, first, rows_ctx)
    q_heads = queries.reshape(rows_ctx, heads_dev, HD)
    scale = HD ** (-0.5)
    start_state = (
        jnp.full((heads_dev, rows_ctx), -1e30, jnp.float32),
        jnp.zeros((heads_dev, rows_ctx), jnp.float32),
        jnp.zeros((rows_ctx, heads_dev, HD), jnp.float32),
    )
    key_rows = lax.all_gather(keys, "ctx", axis=0, tiled=True)
    value_rows = lax.all_gather(values, "ctx", axis=0, tiled=True)
    count = key_rows.shape[0]
    width = 512

    def one_block(step, state):
        best, total, acc = state
        offset = step * width
        key_block = lax.dynamic_slice_in_dim(key_rows, offset, width).reshape(width, heads_dev, HD)
        value_block = lax.dynamic_slice_in_dim(value_rows, offset, width).reshape(
            width, heads_dev, HD
        )
        k_pos = offset + jnp.arange(width, dtype=jnp.int32)
        k_seg = lax.dynamic_slice_in_dim(segments, offset, width)
        allowed = (q_seg[:, None] == k_seg[None, :]) & (k_pos[None, :] <= q_pos[:, None])
        scores = (
            jnp.einsum("qhd,khd->hqk", q_heads, key_block, preferred_element_type=jnp.float32)
            * scale
        )
        scores = jnp.where(allowed[None], scores, jnp.float32(-1e30))
        new_best = jnp.maximum(best, jnp.max(scores, axis=2))
        factor = jnp.exp(best - new_best)
        expo = jnp.where(allowed[None], jnp.exp(scores - new_best[:, :, None]), jnp.float32(0.0))
        total = total * factor + jnp.sum(expo, axis=2)
        update = jnp.einsum(
            "hqk,khd->qhd",
            expo.astype(jnp.bfloat16),
            value_block,
            preferred_element_type=jnp.float32,
        )
        acc = acc * factor.T[:, :, None] + update
        return (new_best, total, acc)

    _, total, acc = lax.fori_loop(0, count // width, one_block, start_state)
    attended = (acc / total.T[:, :, None]).reshape(rows_ctx, width_heads).astype(jnp.bfloat16)
    attn = lax.psum_scatter(
        jnp.dot(attended, out_weight, preferred_element_type=jnp.float32).astype(jnp.bfloat16),
        "ep",
        scatter_dimension=0,
        tiled=True,
    ).astype(jnp.float32)
    stream = residual.astype(jnp.float32) + attn
    normed = (
        stream * lax.rsqrt(jnp.mean(stream * stream, axis=1, keepdims=True) + 1e-06) * norm_gain
    ).astype(jnp.bfloat16)
    logits = jnp.dot(normed.astype(jnp.float32), router, precision=lax.Precision.HIGHEST)
    gates = jax.nn.sigmoid(jnp.take_along_axis(logits, routes, axis=1))
    weights = gates / jnp.sum(gates, axis=1, keepdims=True)
    experts = router.shape[1]
    top_count = routes.shape[1]
    capacity = min(tok_rows, max(2, 2 * tok_rows * top_count // experts))
    exp_ep = experts // n_ep
    slices = n_ctx // exp_ep
    flat = routes.reshape(-1)
    onehot = (flat[:, None] == jnp.arange(experts, dtype=jnp.int32)[None, :]).astype(jnp.int32)
    rank = jnp.sum((jnp.cumsum(onehot, axis=0) - onehot) * onehot, axis=1)
    slot = (flat * capacity + rank).reshape(tok_rows, top_count)
    placed = slot[:, :, None] == jnp.arange(experts * capacity, dtype=jnp.int32)[None, None, :]
    send_table = jnp.any(placed, axis=1).astype(jnp.bfloat16)
    combine = jnp.sum(jnp.where(placed, weights[:, :, None], jnp.float32(0.0)), axis=1)
    buffer = jnp.einsum("tp,td->pd", send_table, normed, preferred_element_type=jnp.float32).astype(
        jnp.bfloat16
    )
    grid = buffer.reshape(n_ep, exp_ep, capacity, model_width)
    gate_local = gate_weight.reshape(model_width, -1)
    up_local = up_weight.reshape(model_width, -1)
    down_local = down_weight.reshape(-1, model_width)
    owned = lax.all_to_all(grid, "ep", split_axis=0, concat_axis=0, tiled=True)
    copies = jnp.repeat(jnp.swapaxes(owned, 0, 1), slices, axis=0)
    arrived = lax.all_to_all(copies, "ctx", split_axis=0, concat_axis=0, tiled=True)
    rows = arrived.reshape(-1, model_width)
    gate = jnp.dot(rows, gate_local, preferred_element_type=jnp.float32)
    upper = jnp.dot(rows, up_local, preferred_element_type=jnp.float32)
    act = (jax.nn.silu(gate) * upper).astype(jnp.bfloat16)
    partial_value = (
        jnp.dot(act, down_local, preferred_element_type=jnp.float32)
        .astype(jnp.bfloat16)
        .reshape(arrived.shape)
    )
    returned = lax.all_to_all(partial_value, "ctx", split_axis=0, concat_axis=0, tiled=True)
    summed = jnp.sum(
        returned.reshape(exp_ep, slices, n_ep, capacity, model_width).astype(jnp.float32), axis=1
    ).astype(jnp.bfloat16)
    back = lax.all_to_all(jnp.swapaxes(summed, 0, 1), "ep", split_axis=0, concat_axis=0, tiled=True)
    expert_rows = back.reshape(-1, model_width)
    mixed = jnp.dot(combine, expert_rows.astype(jnp.float32), precision=lax.Precision.HIGHEST)
    return (stream + mixed).astype(jnp.bfloat16)


NEG = -1e30
LOG2E = 1.4426950408889634
STREAMS = 2


def attend_kernel(where_ref, ids_ref, seg_ref, *refs, planes, rows, part, factor, own):
    n = planes
    q_in, kv_in, refs = refs[:n], refs[n : 2 * n], refs[2 * n :]
    if own:
        acc_ref, stat_ref, q_buf, kv_buf, col_ref, sems = refs
    else:
        acc_in, stat_in, *outs, acc_ref, stat_ref, res_ref, q_buf, kv_buf, col_ref, sems = refs
    z, x, y, core = where_ref[0], where_ref[1], where_ref[2], where_ref[3]
    side = x if own else 1 - x
    copies = []
    for s in range(n):
        copies.append(pltpu.make_async_copy(q_in[s], q_buf.at[s], sems.at[2 * s]))
        copies.append(pltpu.make_async_copy(kv_in[s], kv_buf.at[z ^ s], sems.at[2 * s + 1]))
    for copy in copies:
        copy.start()
    turned = jnp.transpose(seg_ref[...])
    for j in range(2 * n):
        col_ref[j] = turned[:, j : j + 1]
    if own:
        acc_ref[...] = jnp.zeros_like(acc_ref)
    else:
        acc_ref[...] = acc_in[...]
        stat_ref[...] = stat_in[...]
    for copy in copies:
        copy.wait()

    def one_slot(s, carry):
        plane = z ^ s
        block = 2 * plane + x
        query = q_buf[s]
        q_seg = seg_ref[pl.ds(block, 1), :]
        q_pos = block * rows + lax.broadcasted_iota(jnp.int32, (1, rows), 1)

        def step(p, state, masked):
            best, total = state
            key, value = kv_buf[p, 0], kv_buf[p, 1]
            scores = lax.dot_general(
                key, query, (((1,), (1,)), ((), ())), preferred_element_type=jnp.float32
            )
            if masked:
                j = 2 * p + side
                allowed = col_ref[j] == q_seg
                if own:
                    k_pos = j * rows + lax.broadcasted_iota(jnp.int32, (rows, rows), 0)
                    allowed = allowed & (k_pos <= q_pos)
                scores = jnp.where(allowed, scores, NEG)
            new_best = jnp.maximum(best, jnp.max(scores, axis=0, keepdims=True))
            expo = jnp.exp2((scores - new_best) * factor)
            shrink = jnp.exp2((best - new_best) * factor)
            total = total * shrink + jnp.sum(expo, axis=0, keepdims=True)
            update = lax.dot_general(
                value,
                expo.astype(jnp.bfloat16),
                (((0,), (0,)), ((), ())),
                preferred_element_type=jnp.float32,
            )
            acc_ref[s] = acc_ref[s] * shrink + update
            return new_best, total

        low, high = ids_ref[block * rows], ids_ref[block * rows + rows - 1]
        last = plane if own else plane + x
        first, whole = jnp.int32(0), jnp.int32(0)
        for p in range(n):
            start = (2 * p + side) * rows
            first += (ids_ref[start + rows - 1] < low).astype(jnp.int32)
            whole += (ids_ref[start] < high).astype(jnp.int32)
        first, whole = jnp.minimum(first, last), jnp.minimum(whole, last)
        if own:
            state = (jnp.full((1, rows), NEG, jnp.float32), jnp.zeros((1, rows), jnp.float32))
        else:
            stats = stat_ref[s]
            state = (stats[0:1], stats[1:2])
        state = lax.fori_loop(first, whole, functools.partial(step, masked=True), state)
        state = lax.fori_loop(whole, last, functools.partial(step, masked=False), state)
        if own:
            best, total = step(plane, state, True)
            stat_ref[s, 0:1] = best
            stat_ref[s, 1:2] = total
        else:
            res_ref[s] = jnp.transpose(acc_ref[s] / state[1])
        return carry

    lax.fori_loop(0, n, one_slot, 0)
    if own:
        return
    for s in range(n):
        for k in range(2):
            for half in range(2):
                row = pl.multiple_of(((y ^ half) * 2 + (core ^ k)) * part, part)
                outs[2 * s + k][pl.ds(half * part, part), :] = res_ref[
                    s, pl.ds(row, part), :
                ].astype(jnp.bfloat16)


def attend(where, segments, q_in, kv_in, state):
    planes = len(q_in)
    rows = q_in[0].shape[0]
    part = rows // 4
    own = state is None
    any_spec = pl.BlockSpec(memory_space=pl.ANY)
    smem = pl.BlockSpec(memory_space=pltpu.SMEM)
    vmem = pl.BlockSpec(memory_space=pltpu.VMEM)
    kept = [(planes, HD, rows), (planes, 8, rows)]
    if own:
        shapes, states = [jax.ShapeDtypeStruct(k, jnp.float32) for k in kept], []
    else:
        shapes = [jax.ShapeDtypeStruct((2 * part, HD), jnp.bfloat16)] * (2 * planes)
        states = [pltpu.VMEM(k, jnp.float32) for k in kept]
        states.append(pltpu.VMEM((planes, rows, HD), jnp.float32))
    return pl.pallas_call(
        functools.partial(
            attend_kernel,
            planes=planes,
            rows=rows,
            part=part,
            factor=HD ** (-0.5) * LOG2E,
            own=own,
        ),
        out_shape=shapes,
        in_specs=[smem, smem, vmem] + [any_spec] * (2 * planes) + [vmem] * (0 if own else 2),
        out_specs=[vmem] * len(shapes),
        scratch_shapes=states
        + [
            pltpu.VMEM((planes, rows, HD), jnp.bfloat16),
            pltpu.VMEM((planes, 2, rows, HD), jnp.bfloat16),
            pltpu.VMEM((2 * planes, rows, 1), jnp.float32),
            pltpu.SemaphoreType.DMA((2 * planes,)),
        ],
        compiler_params=pltpu.CompilerParams(vmem_limit_bytes=24 << 20),
        cost_estimate=pl.CostEstimate(
            flops=10 * 4 * rows * rows * HD, bytes_accessed=4 << 20, transcendentals=10 * rows * rows
        ),
        name="attend_own" if own else "attend_other",
    )(
        where,
        segments,
        segments.astype(jnp.float32).reshape(2 * planes, rows),
        *q_in,
        *kv_in,
        *([] if own else state),
    )


def split_kernel(where_ref, q_ref, k_ref, v_ref, *outs):
    planes = len(outs) // 2
    for s in reversed(range(planes)):
        lanes = pl.ds(pl.multiple_of((where_ref[0] ^ s) * HD, HD), HD)
        outs[planes + s][0] = k_ref[:, lanes]
        outs[planes + s][1] = v_ref[:, lanes]
        outs[s][...] = q_ref[:, lanes]


def split_heads(where, queries, keys, values):
    rows, width = queries.shape
    planes = width // HD
    vmem = pl.BlockSpec(memory_space=pltpu.VMEM)
    outs = pl.pallas_call(
        split_kernel,
        out_shape=[jax.ShapeDtypeStruct((rows, HD), jnp.bfloat16)] * planes
        + [jax.ShapeDtypeStruct((2, rows, HD), jnp.bfloat16)] * planes,
        in_specs=[pl.BlockSpec(memory_space=pltpu.SMEM)] + [vmem] * 3,
        out_specs=[vmem] * (2 * planes),
        cost_estimate=pl.CostEstimate(
            flops=0, bytes_accessed=12 * rows * width, transcendentals=0
        ),
        name="split_heads",
    )(where, queries, keys, values)
    return outs[:planes], outs[planes:]


def far_kernel(where_ref, *refs, planes):
    pieces, (own_weight, oth_weight, *far, near_out, wide) = refs[: 2 * planes], refs[2 * planes :]
    tok = near_out.shape[0]
    deep = planes * HD
    for k in range(2):
        for s in range(planes):
            piece = pieces[k * planes + s]
            lanes = pl.ds(pl.multiple_of(k * deep + (where_ref[0] ^ s) * HD, HD), HD)
            wide[:, lanes] = piece[tok:]
            near_out[:, lanes] = piece[:tok]
    total = (
        jnp.dot(wide[:, :deep], own_weight[...], preferred_element_type=jnp.float32)
        + jnp.dot(wide[:, deep:], oth_weight[...], preferred_element_type=jnp.float32)
    ).astype(jnp.bfloat16)
    part = tok // len(far)
    for i, out in enumerate(far):
        out[...] = total[i * part : (i + 1) * part]


def project_far(where, pieces, own_weight, oth_weight):
    tok = pieces[0].shape[0] // 2
    deep, wide = own_weight.shape
    vmem = pl.BlockSpec(memory_space=pltpu.VMEM)
    return pl.pallas_call(
        functools.partial(far_kernel, planes=len(pieces) // 2),
        out_shape=[
            jax.ShapeDtypeStruct((tok // STREAMS, wide), jnp.bfloat16),
        ]
        * STREAMS
        + [jax.ShapeDtypeStruct((tok, 2 * deep), jnp.bfloat16)],
        in_specs=[pl.BlockSpec(memory_space=pltpu.SMEM)] + [vmem] * (len(pieces) + 2),
        out_specs=[vmem] * (STREAMS + 1),
        scratch_shapes=[pltpu.VMEM((tok, 2 * deep), jnp.bfloat16)],
        cost_estimate=pl.CostEstimate(
            flops=4 * tok * deep * wide, bytes_accessed=4 * deep * wide, transcendentals=0
        ),
        compiler_params=pltpu.CompilerParams(vmem_limit_bytes=24 << 20),
        name="project_far",
    )(where, *pieces, own_weight, oth_weight)


def near_kernel(attended, own_weight, oth_weight, residual, *outs):
    deep = own_weight.shape[0]
    total = residual[...].astype(jnp.float32) + (
        jnp.dot(attended[:, :deep], own_weight[...], preferred_element_type=jnp.float32)
        + jnp.dot(attended[:, deep:], oth_weight[...], preferred_element_type=jnp.float32)
    )
    part = total.shape[0] // len(outs)
    for i, out in enumerate(outs):
        out[...] = total[i * part : (i + 1) * part]


def project_near(attended, own_weight, oth_weight, residual):
    deep, wide = own_weight.shape
    vmem = pl.BlockSpec(memory_space=pltpu.VMEM)
    return pl.pallas_call(
        near_kernel,
        out_shape=[
            jax.ShapeDtypeStruct((residual.shape[0] // STREAMS, wide), jnp.float32)
        ]
        * STREAMS,
        in_specs=[vmem] * 4,
        out_specs=[vmem] * STREAMS,
        cost_estimate=pl.CostEstimate(
            flops=4 * attended.shape[0] * deep * wide,
            bytes_accessed=4 * deep * wide,
            transcendentals=0,
        ),
        compiler_params=pltpu.CompilerParams(vmem_limit_bytes=24 << 20),
        name="project_near",
    )(attended, own_weight, oth_weight, residual)


def norm_kernel(near, far, gain, stream_out, normed_out):
    stream = near[...] + far[...].astype(jnp.float32)
    stream_out[...] = stream
    mean = jnp.mean(stream * stream, axis=1, keepdims=True)
    normed_out[...] = (stream * lax.rsqrt(mean + 1e-06) * gain[...]).astype(jnp.bfloat16)


def add_norm(near, far, gain):
    vmem = pl.BlockSpec(memory_space=pltpu.VMEM)
    return pl.pallas_call(
        norm_kernel,
        out_shape=[
            jax.ShapeDtypeStruct(near.shape, jnp.float32),
            jax.ShapeDtypeStruct(near.shape, jnp.bfloat16),
        ],
        in_specs=[vmem] * 3,
        out_specs=[vmem] * 2,
        cost_estimate=pl.CostEstimate(
            flops=4 * near.size, bytes_accessed=12 * near.size, transcendentals=near.shape[0]
        ),
        compiler_params=pltpu.CompilerParams(vmem_limit_bytes=24 << 20),
        name="add_norm",
    )(near, far, gain.reshape(1, -1))


def project_down(act_ref, first, down_buf, copies, outs):
    tok, wide = outs[0].shape
    step = wide // len(copies)
    for n, group in enumerate(copies):
        for copy in group:
            copy.wait()
        cols = slice(n * step, (n + 1) * step)
        part = jnp.dot(
            act_ref[first : first + len(outs) * tok, :],
            down_buf[:, cols],
            preferred_element_type=jnp.float32,
        )
        for i, out in enumerate(outs):
            out[:, cols] = part[i * tok : (i + 1) * tok].astype(out.dtype)


def down_shapes(tok, wide, pieces):
    return [jax.ShapeDtypeStruct((tok, wide), jnp.float32)] * (pieces // 2) + [
        jax.ShapeDtypeStruct((tok, wide), jnp.bfloat16)
    ] * (pieces // 2)


def experts_kernel(which_ref, *refs, pieces, slots, experts, half):
    tokens, refs = refs[:pieces], refs[pieces:]
    marks, router_ref, refs = refs[:slots], refs[slots], refs[slots + 1 :]
    weights, refs = refs[:8], refs[8:]
    act_out, outs, refs = refs[0], refs[1 : 1 + pieces // 2], refs[1 + pieces // 2 :]
    rows_ref, up_buf, down_buf, act_ref, all_ref, pick_ref, sems = refs
    tok = tokens[0].shape[0]
    loads = [
        pltpu.make_async_copy(tokens[i], rows_ref.at[pl.ds(i * tok, tok), :], sems.at[9 + i])
        for i in range(pieces)
    ]
    ups = [
        pltpu.make_async_copy(
            weights[2 * i], up_buf.at[pl.ds(2 * i * half, 2 * half), :], sems.at[2 * i]
        )
        for i in range(4)
    ]
    downs = [
        pltpu.make_async_copy(
            weights[2 * i + 1], down_buf.at[pl.ds(i * half, half), :], sems.at[2 * i + 1]
        )
        for i in range(4)
    ]
    for copy in loads + ups[:2]:
        copy.start()
    for copy in loads:
        copy.wait()
    logits = lax.dot_general(
        router_ref[...],
        rows_ref[...],
        (((1,), (1,)), ((), ())),
        preferred_element_type=jnp.float32,
    )
    logits = logits[:experts] + logits[experts : 2 * experts] + logits[2 * experts :]
    group = slots // 2
    mark = jnp.concatenate(
        [
            m[i * experts : (i + 1) * experts, :]
            for first in (0, group)
            for i in range(2)
            for m in marks[first : first + group]
        ],
        axis=1,
    )
    gate = mark / (1.0 + jnp.exp(-logits))
    weight = gate / jnp.sum(gate, axis=0, keepdims=True)
    row = lax.broadcasted_iota(jnp.int32, weight.shape, 0)
    picked = [
        jnp.sum(jnp.where(row == which_ref[i], weight, 0.0), axis=0, keepdims=True)
        for i in range(4)
    ]
    pick_ref[...] = jnp.transpose(jnp.concatenate(picked + picked, axis=0))
    rows = pieces * tok
    ready = 0
    for first in range(0, rows, rows // 2):
        block = slice(first, first + rows // 2)
        for low in range(0, 8 * half, 512):
            high = min(low + 512, 8 * half)
            while ready * 2 * half < high and ready < 4:
                ups[ready].wait()
                for copy in ups[ready + 2 :][:1] if ready < 2 else downs[2 * ready - 4 :][:2]:
                    copy.start()
                ready += 1
            all_ref[:, low:high] = lax.dot_general(
                rows_ref[block, :],
                up_buf[low:high, :],
                (((1,), (1,)), ((), ())),
                preferred_element_type=jnp.float32,
            )
        for i in range(4):
            a = all_ref[:, 2 * i * half : (2 * i + 1) * half]
            b = all_ref[:, (2 * i + 1) * half : (2 * i + 2) * half]
            act_ref[block, i * half : (i + 1) * half] = (
                a / (1.0 + jnp.exp(-a)) * b * pick_ref[block, i : i + 1]
            ).astype(jnp.bfloat16)
    store = pltpu.make_async_copy(act_ref.at[pl.ds(0, rows // 2), :], act_out, sems.at[8])
    store.start()
    project_down(act_ref, rows // 2, down_buf, [downs, [], [], []], outs)
    store.wait()


def run_experts(which, tokens, marks, router_parts, weights, experts):
    pieces = len(tokens)
    tok, wide = tokens[0].shape
    half = weights[1].shape[0]
    rows = pieces * tok
    vmem = pl.BlockSpec(memory_space=pltpu.VMEM)
    anywhere = pl.BlockSpec(memory_space=pl.ANY)
    act, *outs = pl.pallas_call(
        functools.partial(
            experts_kernel, pieces=pieces, slots=len(marks), experts=experts, half=half
        ),
        out_shape=[jax.ShapeDtypeStruct((rows // 2, 4 * half), jnp.bfloat16)]
        + down_shapes(tok, wide, pieces // 2),
        in_specs=[pl.BlockSpec(memory_space=pltpu.SMEM)]
        + [anywhere] * pieces
        + [vmem] * (len(marks) + 1)
        + [anywhere] * 8,
        out_specs=[anywhere] + [vmem] * (pieces // 2),
        scratch_shapes=[
            pltpu.VMEM((rows, wide), jnp.bfloat16),
            pltpu.VMEM((8 * half, wide), jnp.bfloat16),
            pltpu.VMEM((4 * half, wide), jnp.bfloat16),
            pltpu.VMEM((rows, 4 * half), jnp.bfloat16),
            pltpu.VMEM((rows // 2, 8 * half), jnp.float32),
            pltpu.VMEM((rows, 8), jnp.float32),
            pltpu.SemaphoreType.DMA((9 + pieces,)),
        ],
        cost_estimate=pl.CostEstimate(
            flops=5 * rows * wide * half * 4,
            bytes_accessed=6 * wide * half * 4,
            transcendentals=rows * half * 4,
        ),
        name="experts",
    )(which, *tokens, *marks, router_parts, *weights)
    return act, outs


def down_kernel(act_ref, *refs, half):
    weights, outs, (down_buf, sems) = refs[:4], refs[4:-2], refs[-2:]
    step = down_buf.shape[1] // 4
    copies = [
        [
            pltpu.make_async_copy(
                weights[i].at[:, pl.ds(n * step, step)],
                down_buf.at[pl.ds(i * half, half), pl.ds(n * step, step)],
                sems.at[4 * n + i],
            )
            for i in range(4)
        ]
        for n in range(4)
    ]
    for group in copies:
        for copy in group:
            copy.start()
    project_down(act_ref, 0, down_buf, copies, outs)


def finish_experts(act, weights, pieces):
    rows = act.shape[0]
    half, wide = weights[0].shape
    return pl.pallas_call(
        functools.partial(down_kernel, half=half),
        out_shape=down_shapes(rows // pieces, wide, pieces),
        in_specs=[pl.BlockSpec(memory_space=pltpu.VMEM)] + [pl.BlockSpec(memory_space=pl.ANY)] * 4,
        out_specs=[pl.BlockSpec(memory_space=pltpu.VMEM)] * pieces,
        scratch_shapes=[
            pltpu.VMEM((4 * half, wide), jnp.bfloat16),
            pltpu.SemaphoreType.DMA((16,)),
        ],
        cost_estimate=pl.CostEstimate(
            flops=2 * rows * wide * half * 4,
            bytes_accessed=2 * wide * half * 4,
            transcendentals=0,
        ),
        name="finish_experts",
    )(act, *weights)


def dense_body(
    queries,
    keys,
    values,
    segments,
    residual,
    out_weight,
    norm_gain,
    router,
    routes,
    gate_weight,
    up_weight,
    down_weight,
):
    n_ctx = lax.axis_size("ctx")
    n_ep = lax.axis_size("ep")
    planes = n_ctx // 2
    ctx, ep = lax.axis_index("ctx"), lax.axis_index("ep")
    z, x, y, core = ctx // 2, ctx % 2, ep // 2, ep % 2
    experts = router.shape[1]
    exp_ep = experts // n_ep
    slices = n_ctx // exp_ep

    def over_x(v):
        return lax.ppermute(v, "ctx", [(c, c ^ 1) for c in range(n_ctx)])

    def over_z(v, s):
        return lax.ppermute(v, "ctx", [(c, c ^ (2 * s)) for c in range(n_ctx)])

    def along_z(v, pairs):
        return lax.ppermute(v, "ctx", [(2 * a + i, 2 * b + i) for a, b in pairs for i in range(2)])

    def over_y(v):
        return lax.ppermute(v, "ep", [(e, e ^ 2) for e in range(n_ep)])

    def over_core(v):
        return lax.ppermute(v, "ep", [(e, e ^ 1) for e in range(n_ep)])

    def over_z_core(v, s, k):
        pairs = [
            (c * n_ep + e, (c ^ (2 * s)) * n_ep + (e ^ k)) for c in range(n_ctx) for e in range(n_ep)
        ]
        return lax.ppermute(v, ("ctx", "ep"), pairs)

    where = jnp.stack([z, x, y, core])

    q_send, kv_send = split_heads(where, queries, keys, values)
    kv_own, q_in = [None] * planes, [None] * planes
    for s in reversed(range(planes)):
        kv_own[s] = over_z(kv_send[s], s) if s else kv_send[s]
    for s in reversed(range(planes)):
        q_in[s] = over_z(q_send[s], s) if s else q_send[s]
    kv_oth = []
    for s in range(planes):
        kv_oth.append(over_x(kv_own[s]))

    def gather_ep(w):
        far = over_y(w)
        near_other = over_core(w)
        far_other = over_core(far)
        return [w, near_other, far, far_other]

    def rows_first(w):
        return jnp.swapaxes(w.reshape(w.shape[2:]), 0, 1)

    up_all = gather_ep(jnp.concatenate([rows_first(gate_weight), rows_first(up_weight)]))
    down_all = gather_ep(down_weight.reshape(down_weight.shape[2:]))
    weights = [w for pair in zip(up_all, down_all) for w in pair]
    out_oth = over_core(out_weight)

    expert_ids = jnp.arange(experts, dtype=jnp.int32)
    mark = jnp.any(routes.T[:, None, :] == expert_ids[None, :, None], axis=0).astype(jnp.float32)
    mark = jnp.concatenate([mark, over_x(mark)])
    marks = [mark]
    for s in range(1, planes):
        marks.append(over_z(mark, s))
    outer = (z == 0) | (z == planes - 1)
    marks[2:] = [jnp.where(outer, marks[2], marks[3]), jnp.where(outer, marks[3], marks[2])]

    state = attend(where, segments, q_in, kv_own, None)
    outs = attend(where, segments, q_in, kv_oth, state)
    pieces = []
    for k in range(2):
        for s in range(planes):
            piece = outs[2 * s + k]
            pieces.append(piece if s == 0 and k == 0 else over_z_core(piece, s, k))
    *far_parts, attended = project_far(where, pieces, out_weight, out_oth)
    far = []
    for h in range(STREAMS):
        far.append(over_y(far_parts[h]))
    near = project_near(attended, out_weight, out_oth, residual)

    inner = [(1, 2), (2, 1)]
    stream, own, oth = [], [], []
    for h in range(STREAMS):
        kept, normed = add_norm(near[h], far[h], norm_gain)
        stream.append(kept)
        tok1 = over_z(normed, 1)
        tok2 = along_z(normed, inner)
        tok3 = along_z(tok1, inner)
        tok2 = jnp.where(outer, over_z(tok2, 1), tok2)
        tok3 = jnp.where(outer, over_z(tok3, 1), tok3)
        own.append((normed, tok1, tok2, tok3))
        others = []
        for k in range(4):
            others.append(over_x(own[h][k]))
        oth.append(others)

    parts = []
    left = router
    for _ in range(3):
        cut = lax.reduce_precision(left, 8, 7)
        parts.append(cut.astype(jnp.bfloat16))
        left = left - cut
    router_parts = jnp.concatenate([part.T for part in parts])
    which = jnp.stack([w * exp_ep + ctx // slices for w in (ep, ep ^ 1, ep ^ 2, ep ^ 3)])

    def of_slots(pair, sides=(own, oth)):
        return [side[h][k] for side in sides for k in pair for h in range(STREAMS)]

    keep, back = [None] * 4, [None] * 4

    def deal(pair, outs):
        for i, k in enumerate(pair):
            keep[k] = outs[i * STREAMS : (i + 1) * STREAMS]
            back[k] = outs[(2 + i) * STREAMS : (3 + i) * STREAMS]

    near_slots, far_slots = (0, 1), (2, 3)
    act, outs = run_experts(
        which, of_slots(near_slots) + of_slots(far_slots), marks, router_parts, weights, experts
    )
    deal(far_slots, outs)
    deal(near_slots, finish_experts(act, down_all, 4 * STREAMS))

    def wide(v):
        return v.astype(jnp.float32)

    def send(v):
        return v.astype(jnp.bfloat16)

    def from_outer(v):
        return jnp.where(outer, 0.0, wide(over_z(send(v), 1)))

    result = []
    for h in range(STREAMS):
        sums = [None] * 4
        for k in (3, 2, 1, 0):
            sums[k] = keep[k][h] + wide(over_x(back[k][h]))
        got = from_outer(sums[3])
        got = wide(along_z(send(sums[3] + got), inner))
        mid = from_outer(sums[2])
        mid = wide(along_z(send(sums[2] + mid), inner))
        last = wide(over_z(send(sums[1] + got), 1))
        result.append(send(stream[h] + (sums[0] + mid + last)))
    return jnp.concatenate(result)


def body(*arrays):
    queries, residual, router, routes = arrays[0], arrays[4], arrays[7], arrays[8]
    n_ctx, n_ep = lax.axis_size("ctx"), lax.axis_size("ep")
    rows_all = residual.shape[0] * routes.shape[1]
    dense = 4 * rows_all >= 3 * residual.shape[0] * router.shape[1]
    shaped = n_ctx == 8 and n_ep == 4 and queries.shape[1] == n_ctx // 2 * HD
    if dense and shaped:
        return dense_body(*arrays)
    return general_body(*arrays)


def solution(mesh):
    placed = (
        P("ctx", "ep"),
        P("ctx", "ep"),
        P("ctx", "ep"),
        P(),
        P(("ctx", "ep"), None),
        P("ep", None),
        P(),
        P(),
        P(("ctx", "ep"), None),
        P("ep", "ctx", None, None),
        P("ep", "ctx", None, None),
        P("ep", "ctx", None, None),
    )
    return jax.shard_map(
        body, mesh=mesh, in_specs=placed, out_specs=P(("ctx", "ep"), None), check_vma=False
    )
```
